128 devices in a mesh: fr: 4 (over x_hi, core), fc: 32 (over z, x_lo, y).
Axes of the slice: x: 4 (x_hi: 2, x_lo: 2; x = x_hi * 2 + x_lo), y: 4, z: 4, core: 2. Of those that a mesh axis runs over, the one named last changes fastest.
Arguments:
- front_slab: float32 [2048, 98304], P('fr', 'fc'), may hold values from -6 to 6
- panels: float32 [4, 98304, 256], P(None, 'fc'), may hold values from -8 to 8
- diagonal_blocks: float32 [4, 256, 256], P(None, None, 'fc'), may hold values from -3 to 96, as said below
- extend_maps: int32 [4, 4, 32, 128], P(None, 'fr', 'fc'), may hold values from 0 to 127, each once within a row
Outputs:
- front_out: float32 [2048, 98304], P('fr', 'fc')
The draws below stay inside these ranges and needn't reach their ends.
Inputs may be any that keep to these rules, and one draw needn't show every extreme that they name: `extend_maps`: each level's map at each grid position names every row of the block once. `diagonal_blocks`: the symmetric part of each block is positive definite.
All inputs are finite; a program needn't handle non-finite values.
Results may differ from the reference program's by a relative error of at most 0.0001.
Values sent between devices are 32-bit elements; how exact they have to be, the bound alone decides.
No kernel may reach another device: no remote copies, remote signals or barrier semaphores. Data moves between devices by JAX's collectives and lax.ppermute only.
A program may use at most 128 MiB of HBM per device.

```python
import jax
import jax.numpy as jnp
import numpy as np
from jax import lax

LEVELS = 4
PW = 256
BLOCK = 128
CD = 3072
RD = 512
NT = 98304
SLAB = 2048
N_FR = 4
N_FC = 32


def draw_diagonal_blocks(key, part):
    key_values, key_scales = jax.random.split(jax.random.fold_in(key, 11))
    values = jnp.clip(jax.random.normal(key_values, (LEVELS, PW, PW), jnp.float32), -3.0, 3.0)
    scales = jax.random.uniform(key_scales, (LEVELS, PW), jnp.float32, 48.0, 96.0)
    identity = jnp.eye(PW, dtype=jnp.float32)
    return values * (1.0 - identity) + scales[:, None, :] * identity


def level_of(rng, shape, cuts, low, largest):
    loudness, own = 1.0, jax.random.fold_in(rng, 6)
    for dim, parts in cuts:
        draws = jnp.exp(jax.random.uniform(jax.random.fold_in(own, dim), (parts,), jnp.float32, low / len(cuts), largest / len(cuts)))
        loudness = loudness * jnp.repeat(draws, shape[dim] // parts).reshape([-1 if axis == dim else 1 for axis in range(len(shape))])
    return loudness


def noise(rng, extent, deviation, reach, pieces=(), kind=jnp.bfloat16):
    values = deviation * jax.random.normal(rng, extent, jnp.float32)
    if pieces:
        values = values * level_of(rng, extent, pieces, -0.22, 0.18)
    return jnp.clip(values, -reach, reach).astype(kind)


def setup_inputs(seed: int = 0) -> dict:
    keys = jax.random.split(jax.random.key(seed), 5)
    return {
        "front_slab": noise(keys[0], (SLAB, NT), 1.0, 6.0, ((0, 4), (1, 32)), jnp.float32),
        "panels": noise(keys[1], (LEVELS, NT, PW), 1.5, 8.0, ((1, 32),), jnp.float32),
        "diagonal_blocks": draw_diagonal_blocks(jax.random.fold_in(keys[4], 71), 0),
        "extend_maps": jax.vmap(lambda own: jax.random.permutation(own, BLOCK))(jax.random.split(keys[3], LEVELS * N_FR * N_FC)).reshape((LEVELS, N_FR, N_FC, BLOCK)).astype(jnp.int32),
    }


HIGHEST = lax.Precision.HIGHEST

def inverse_factor(diagonal_block):
    symmetric = 0.5 * (diagonal_block + diagonal_block.T)
    lower_factor = jnp.linalg.cholesky(symmetric)
    identity = jnp.eye(symmetric.shape[0], dtype=symmetric.dtype)
    return lax.linalg.triangular_solve(lower_factor, identity, left_side=True, lower=True)

def reference(front_slab, panels, diagonal_blocks, extend_maps):
    partner_plan = [(True, N_FC // 2), (True, 1), (False, N_FR // 2), (False, 1)]
    for level_index in range(LEVELS):
        grid_view = front_slab.reshape(N_FR, RD, N_FC, CD)
        top_rows = jnp.transpose(grid_view[:, :BLOCK], (0, 2, 1, 3))
        use_columns, flip_mask = partner_plan[level_index]
        if use_columns:
            partner_top = top_rows[:, np.arange(N_FC) ^ flip_mask]
        else:
            partner_top = top_rows[np.arange(N_FR) ^ flip_mask]
        row_map = jnp.broadcast_to(extend_maps[level_index][..., None], partner_top.shape)
        merged = top_rows + jnp.take_along_axis(partner_top, row_map, axis=2)
        grid_view = grid_view.at[:, :BLOCK].set(jnp.transpose(merged, (0, 2, 1, 3)))
        front_slab = grid_view.reshape(SLAB, NT)
        inverse = inverse_factor(diagonal_blocks[level_index])
        column_factor = jnp.dot(panels[level_index], inverse.T, precision=HIGHEST)
        front_slab = front_slab - jnp.dot(column_factor[:SLAB], column_factor.T, precision=HIGHEST)
    return front_slab
```

```python
import functools

import jax
import jax.numpy as jnp
from jax import lax
from jax.experimental import pallas as pl
from jax.experimental.pallas import tpu as pltpu
from jax.sharding import PartitionSpec as P

BF16, F32 = jnp.bfloat16, jnp.float32

def split3(x):
    hi = x.astype(BF16)
    rest = x - hi.astype(F32)
    mid = rest.astype(BF16)
    low = (rest - mid.astype(F32)).astype(BF16)
    return hi, mid, low

def dot_nt(a, b):
    return lax.dot_general(a, b, (((1,), (1,)), ((), ())), preferred_element_type=F32)

def product_nt(a, b):
    ah, am, al = split3(a)
    bh, bm, bl = split3(b)
    cat = lambda x, y: jnp.concatenate([x, y], axis=1)
    small = dot_nt(cat(am, ah), cat(bm, bl)) + dot_nt(cat(al, am), cat(bh, bh))
    return dot_nt(cat(ah, ah), cat(bh, bm)) + small

def sweep_block(block, width):
    rows, lanes = block.shape
    row = lax.broadcasted_iota(jnp.int32, (rows, lanes), 0)
    lane = lax.broadcasted_iota(jnp.int32, (rows, lanes), 1)
    own = lane % width
    group = lane - own
    own1 = own[:1]
    for p in range(0, rows, 2):
        c0 = jnp.take_along_axis(block, group + p, axis=1)
        c1 = jnp.take_along_axis(block, group + (p + 1), axis=1)
        d00, d01, d11 = c0[p:p + 1], c0[p + 1:p + 2], c1[p + 1:p + 2]
        r0 = jnp.where(own1 == p, -1.0, jnp.where(own1 == p + 1, 0.0, block[p:p + 1]))
        r1 = jnp.where(own1 == p + 1, -1.0, jnp.where(own1 == p, 0.0, block[p + 1:p + 2]))
        scale = 1.0 / (d00 * d11 - d01 * d01)
        u0 = (d11 * r0 - d01 * r1) * scale
        u1 = (d00 * r1 - d01 * r0) * scale
        at0, at1 = row == p, row == p + 1
        c0 = jnp.where(at0, -1.0, jnp.where(at1, 0.0, c0))
        c1 = jnp.where(at1, -1.0, jnp.where(at0, 0.0, c1))
        pivot = at0 | at1 | (own == p) | (own == p + 1)
        block = jnp.where(pivot, 0.0, block) - c0 * u0 - c1 * u1
    return block

def inverse_kernel(gathered_ref, inverse_ref, packed_ref, *, width):
    levels, order = inverse_ref.shape[0], inverse_ref.shape[1]
    lanes = levels * width
    blocks = order // width
    per_tile = lanes // width
    lane_group = lax.broadcasted_iota(jnp.int32, (order, lanes), 1) // width
    for level in range(levels):
        rows = gathered_ref[:, level].reshape(order, order)
        symmetric = 0.5 * (rows + rows.T)
        for b in range(blocks):
            tile, place = divmod(b, per_tile)
            piece = symmetric[:, tile * lanes:(tile + 1) * lanes]
            shift = (level - place) * width % lanes
            if shift:
                piece = pltpu.roll(piece, shift, 1)
            cols = slice(b * lanes, (b + 1) * lanes)
            if level == 0:
                packed_ref[:, cols] = piece
            else:
                packed_ref[:, cols] = jnp.where(lane_group == level, piece, packed_ref[:, cols])
    same = (lax.broadcasted_iota(jnp.int32, (lanes, lanes), 0) // width
            == lax.broadcasted_iota(jnp.int32, (lanes, lanes), 1) // width)
    small_row = lax.broadcasted_iota(jnp.int32, (width, lanes), 0)
    small_own = lax.broadcasted_iota(jnp.int32, (width, lanes), 1) % width
    minus_identity = jnp.where(small_row == small_own, -1.0, 0.0)

    def spread(x):
        return jnp.where(same, jnp.concatenate([x] * levels, axis=0), 0.0)

    def step(b, carry):
        cols = pl.ds(pl.multiple_of(b * lanes, lanes), lanes)
        rows = pl.ds(pl.multiple_of(b * width, width), width)
        negated = sweep_block(packed_ref[rows, cols], width)
        packed_ref[rows, :] = jnp.zeros((width, blocks * lanes), F32)
        packed_ref[rows, cols] = minus_identity
        column = packed_ref[:, cols]
        packed_ref[:, cols] = jnp.zeros((order, lanes), F32)
        scaled = product_nt(column, spread(negated))
        wide = jnp.concatenate(
            [spread(column[i * width:(i + 1) * width]) for i in range(blocks)], axis=0)
        packed_ref[...] += product_nt(scaled, wide)
        return carry

    lax.fori_loop(0, blocks, step, 0)
    for level in range(levels):
        for tile in range(order // lanes):
            total = None
            for place in range(per_tile):
                b = tile * per_tile + place
                piece = packed_ref[:, b * lanes:(b + 1) * lanes]
                shift = (place - level) * width % lanes
                if shift:
                    piece = pltpu.roll(piece, shift, 1)
                total = piece if total is None else jnp.where(lane_group == place, piece, total)
            inverse_ref[level, :, tile * lanes:(tile + 1) * lanes] = -total

def inverses(gathered):
    parts, levels, eight, order = gathered.shape
    width = 32
    return pl.pallas_call(
        functools.partial(inverse_kernel, width=width),
        out_shape=jax.ShapeDtypeStruct((levels, order, order), F32),
        in_specs=[pl.BlockSpec(memory_space=pltpu.VMEM)],
        out_specs=pl.BlockSpec(memory_space=pltpu.VMEM),
        scratch_shapes=[pltpu.VMEM((order, levels * order), F32)],
        compiler_params=pltpu.CompilerParams(vmem_limit_bytes=40 << 20),
        name="symmetric_inverses",
    )(gathered)


def rows_kernel(tops_ref, window_ref, inverse_ref, high_ref, low_ref, other_high_ref, other_low_ref):
    level = pl.program_id(0)
    top = tops_ref.shape[1]

    def product(x):
        y = product_nt(x, inverse_ref[0])
        high = y.astype(BF16)
        return high, (y - high.astype(F32)).astype(BF16)

    rows = jnp.concatenate([tops_ref[level], window_ref[0, top:]], axis=0)
    high_ref[...], low_ref[...] = product(rows)

    @pl.when(level == 0)
    def _():
        other_high_ref[...], other_low_ref[...] = product(tops_ref[tops_ref.shape[0] - 1])


def solved_rows(tops, window, inverse):
    levels, rows, width = window.shape
    top = tops.shape[1]
    wide = jax.ShapeDtypeStruct((rows, levels * width), BF16)
    other = jax.ShapeDtypeStruct((top, width), BF16)
    return pl.pallas_call(
        rows_kernel,
        grid=(levels,),
        out_shape=(wide, wide, other, other),
        in_specs=[
            pl.BlockSpec(tops.shape, lambda l: (0, 0, 0)),
            pl.BlockSpec((1, rows, width), lambda l: (l, 0, 0)),
            pl.BlockSpec((1, width, width), lambda l: (l, 0, 0)),
        ],
        out_specs=(
            pl.BlockSpec((rows, width), lambda l: (0, l)),
            pl.BlockSpec((rows, width), lambda l: (0, l)),
            pl.BlockSpec((top, width), lambda l: (0, 0)),
            pl.BlockSpec((top, width), lambda l: (0, 0)),
        ),
        name="solved_rows",
    )(tops, window, inverse)


def update_kernel(
    core_ref, front_ref, merged_ref, panels_ref, near_ref, far_ref, high_ref, low_ref,
    other_high_ref, other_low_ref, out_ref, *, tiles,
):
    levels = panels_ref.shape[0]
    top = merged_ref.shape[0]
    half = pl.program_id(0) // (tiles // 2)

    def split2(x):
        high = x.astype(BF16)
        return high, (x - high.astype(F32)).astype(BF16)

    def product(high, low, x):
        x_high, x_low = split2(x)
        return dot_nt(high, x_high) + (dot_nt(high, x_low) + dot_nt(low, x_high))

    columns = jnp.concatenate([panels_ref[l] for l in range(levels)], axis=1)
    update = product(high_ref[...], low_ref[...], columns)
    partner = jnp.where(half == core_ref[0], near_ref[...], far_ref[...])
    partner_update = product(other_high_ref[...], other_low_ref[...], partner)
    out_ref[:top] = merged_ref[...] - (update[:top] + partner_update)
    out_ref[top:] = front_ref[top:] - update[top:]


def updated_front(core, front, merged, panels, near, far, high, low, other_high, other_low):
    rows, cols = front.shape
    top = merged.shape[0]
    levels, _, width = panels.shape
    tile = 256
    tiles = cols // tile
    whole = lambda x: pl.BlockSpec(x.shape, lambda j, core: (0, 0))
    half = pl.BlockSpec((tile, width), lambda j, core: (lax.rem(j, tiles // 2), 0))
    return pl.pallas_call(
        functools.partial(update_kernel, tiles=tiles),
        grid_spec=pltpu.PrefetchScalarGridSpec(
            num_scalar_prefetch=1,
            grid=(tiles,),
            in_specs=[
                pl.BlockSpec((rows, tile), lambda j, core: (0, j)),
                pl.BlockSpec((top, tile), lambda j, core: (0, j)),
                pl.BlockSpec((levels, tile, width), lambda j, core: (0, j, 0)),
                half,
                half,
                whole(high),
                whole(low),
                whole(other_high),
                whole(other_low),
            ],
            out_specs=pl.BlockSpec((rows, tile), lambda j, core: (0, j)),
        ),
        out_shape=jax.ShapeDtypeStruct(front.shape, F32),
        compiler_params=pltpu.CompilerParams(vmem_limit_bytes=40 << 20),
        name="updated_front",
    )(core, front, merged, panels, near, far, high, low, other_high, other_low)


def partner(x, axis, flip):
    return lax.ppermute(x, axis, [(i, i ^ flip) for i in range(lax.axis_size(axis))])


def moved(x, row_map):
    return jnp.take(x, row_map, axis=0, mode="clip")


def to_all(x, axis):
    copies = jnp.broadcast_to(x[None], (lax.axis_size(axis), *x.shape))
    return lax.all_to_all(copies, axis, 0, 0, tiled=True)


def body(front, panels, diagonal_blocks, extend_maps):
    rows, cols = front.shape
    levels, _, width = panels.shape
    top = extend_maps.shape[3]
    row_index = lax.axis_index("fr")
    row_devices, col_devices = lax.axis_size("fr"), lax.axis_size("fc")
    maps = [extend_maps[l, 0, 0] for l in range(levels)]

    gathered = to_all(jnp.swapaxes(diagonal_blocks, 1, 2), "fc")
    own = lax.dynamic_slice_in_dim(panels, row_index * rows, rows, 1)
    own = own.reshape(levels * rows, width)
    piece = lax.all_to_all(own, "fc", 0, 0, tiled=True)[:own.shape[0] // col_devices]
    window = to_all(piece, "fc").reshape(levels, rows, width)

    core = row_index % 2
    half = cols // 2
    near = partner(lax.dynamic_slice_in_dim(panels[0], core * half, half, 0), "fc", 1)
    far = partner(near, "fr", 1)

    merged = front[:top]
    flips = [("fc", col_devices // 2), ("fc", 1), ("fr", row_devices // 2), ("fr", 1)]
    for (axis, flip), row_map in zip(flips, maps):
        merged = merged + moved(partner(merged, axis, flip), row_map)

    inverse = inverses(gathered)

    first = window[:, :top]
    lefts = jnp.concatenate([first[0], first[1], moved(first[0], maps[1])], axis=1)
    lefts = lefts + moved(partner(lefts, *flips[2]), maps[2])
    lefts = jnp.concatenate([lefts, first[2]], axis=1)
    lefts = lefts + moved(partner(lefts, *flips[3]), maps[3])
    zero, one, other, two = [lefts[:, i * width:(i + 1) * width] for i in range(4)]
    tops = jnp.stack([zero, one, two, first[3], other])

    high, low, other_high, other_low = solved_rows(tops, window, inverse)
    return updated_front(
        core[None], front, merged, panels, near, far, high, low, other_high, other_low)


def solution(mesh):
    in_specs = (P("fr", "fc"), P(None, "fc", None), P(None, None, "fc"), P(None, "fr", "fc", None))
    out_specs = P("fr", "fc")
    return jax.shard_map(body, mesh=mesh, in_specs=in_specs, out_specs=out_specs, check_vma=False)
```

```python
import functools

import jax
import jax.numpy as jnp
from jax import lax
from jax.experimental import pallas as pl
from jax.experimental.pallas import tpu as pltpu
from jax.sharding import PartitionSpec as P

BF16, F32 = jnp.bfloat16, jnp.float32
COST = pl.CostEstimate(flops=1, bytes_accessed=1, transcendentals=0)

def split3(x):
    hi = x.astype(BF16)
    rest = x - hi.astype(F32)
    mid = rest.astype(BF16)
    low = (rest - mid.astype(F32)).astype(BF16)
    return hi, mid, low

def dot_nt(a, b):
    return lax.dot_general(a, b, (((1,), (1,)), ((), ())), preferred_element_type=F32)

def product_nt(a, b):
    ah, am, al = split3(a)
    bh, bm, bl = split3(b)
    cat = lambda x, y: jnp.concatenate([x, y], axis=1)
    small = dot_nt(cat(am, ah), cat(bm, bl)) + dot_nt(cat(al, am), cat(bh, bh))
    return dot_nt(cat(ah, ah), cat(bh, bm)) + small

def sweep_block(block, width):
    rows, lanes = block.shape
    row = lax.broadcasted_iota(jnp.int32, (rows, lanes), 0)
    lane = lax.broadcasted_iota(jnp.int32, (rows, lanes), 1)
    own = lane % width
    group = lane - own
    own1 = own[:1]
    for p in range(0, rows, 2):
        c0 = jnp.take_along_axis(block, group + p, axis=1)
        c1 = jnp.take_along_axis(block, group + (p + 1), axis=1)
        d00, d01, d11 = c0[p:p + 1], c0[p + 1:p + 2], c1[p + 1:p + 2]
        r0 = jnp.where(own1 == p, -1.0, jnp.where(own1 == p + 1, 0.0, block[p:p + 1]))
        r1 = jnp.where(own1 == p + 1, -1.0, jnp.where(own1 == p, 0.0, block[p + 1:p + 2]))
        scale = 1.0 / (d00 * d11 - d01 * d01)
        u0 = (d11 * r0 - d01 * r1) * scale
        u1 = (d00 * r1 - d01 * r0) * scale
        at0, at1 = row == p, row == p + 1
        c0 = jnp.where(at0, -1.0, jnp.where(at1, 0.0, c0))
        c1 = jnp.where(at1, -1.0, jnp.where(at0, 0.0, c1))
        pivot = at0 | at1 | (own == p) | (own == p + 1)
        block = jnp.where(pivot, 0.0, block) - c0 * u0 - c1 * u1
    return block

def inverse_kernel(gathered_ref, inverse_ref, packed_ref, *, width):
    levels, order = inverse_ref.shape[0], inverse_ref.shape[1]
    lanes = levels * width
    blocks = order // width
    per_tile = lanes // width
    lane_group = lax.broadcasted_iota(jnp.int32, (order, lanes), 1) // width
    for level in range(levels):
        rows = gathered_ref[:, level].reshape(order, order)
        symmetric = 0.5 * (rows + rows.T)
        for b in range(blocks):
            tile, place = divmod(b, per_tile)
            piece = symmetric[:, tile * lanes:(tile + 1) * lanes]
            shift = (level - place) * width % lanes
            if shift:
                piece = pltpu.roll(piece, shift, 1)
            cols = slice(b * lanes, (b + 1) * lanes)
            if level == 0:
                packed_ref[:, cols] = piece
            else:
                packed_ref[:, cols] = jnp.where(lane_group == level, piece, packed_ref[:, cols])
    same = (lax.broadcasted_iota(jnp.int32, (lanes, lanes), 0) // width
            == lax.broadcasted_iota(jnp.int32, (lanes, lanes), 1) // width)
    small_row = lax.broadcasted_iota(jnp.int32, (width, lanes), 0)
    small_own = lax.broadcasted_iota(jnp.int32, (width, lanes), 1) % width
    minus_identity = jnp.where(small_row == small_own, -1.0, 0.0)

    def spread(x):
        return jnp.where(same, jnp.concatenate([x] * levels, axis=0), 0.0)

    def step(b, carry):
        cols = pl.ds(pl.multiple_of(b * lanes, lanes), lanes)
        rows = pl.ds(pl.multiple_of(b * width, width), width)
        negated = sweep_block(packed_ref[rows, cols], width)
        packed_ref[rows, :] = jnp.zeros((width, blocks * lanes), F32)
        packed_ref[rows, cols] = minus_identity
        column = packed_ref[:, cols]
        packed_ref[:, cols] = jnp.zeros((order, lanes), F32)
        scaled = product_nt(column, spread(negated))
        wide = jnp.concatenate(
            [spread(column[i * width:(i + 1) * width]) for i in range(blocks)], axis=0)
        packed_ref[...] += product_nt(scaled, wide)
        return carry

    lax.fori_loop(0, blocks, step, 0)
    for level in range(levels):
        for tile in range(order // lanes):
            total = None
            for place in range(per_tile):
                b = tile * per_tile + place
                piece = packed_ref[:, b * lanes:(b + 1) * lanes]
                shift = (place - level) * width % lanes
                if shift:
                    piece = pltpu.roll(piece, shift, 1)
                total = piece if total is None else jnp.where(lane_group == place, piece, total)
            inverse_ref[level, :, tile * lanes:(tile + 1) * lanes] = -total

def inverses(gathered):
    parts, levels, eight, order = gathered.shape
    width = 32
    return pl.pallas_call(
        functools.partial(inverse_kernel, width=width),
        out_shape=jax.ShapeDtypeStruct((levels, order, order), F32),
        in_specs=[pl.BlockSpec(memory_space=pltpu.VMEM)],
        out_specs=pl.BlockSpec(memory_space=pltpu.VMEM),
        scratch_shapes=[pltpu.VMEM((order, levels * order), F32)],
        compiler_params=pltpu.CompilerParams(vmem_limit_bytes=16 << 20),
        cost_estimate=COST,
        name="symmetric_inverses",
    )(gathered)


def split2(x):
    high = x.astype(BF16)
    return high, (x - high.astype(F32)).astype(BF16)


def product2_nt(a, b):
    return dot_nt(a[0], b[0]) + (dot_nt(a[0], b[1]) + dot_nt(a[1], b[0]))


def moved(x, row_map):
    rows = x.shape[0]
    pick = lax.broadcasted_iota(jnp.int32, (rows, rows), 0) == row_map
    pick = jnp.where(pick, 1.0, 0.0).T.astype(BF16)
    high, mid, low = (jnp.dot(pick, part, preferred_element_type=F32) for part in split3(x))
    return (high + mid) + low


def merge_kernel(own_ref, received_ref, map_ref, out_ref):
    step = 256
    for start in range(0, out_ref.shape[1], step):
        cols = slice(start, start + step)
        out_ref[:, cols] = own_ref[:, cols] + moved(received_ref[:, cols], map_ref[...])


def merge(own, received, row_map):
    return pl.pallas_call(
        merge_kernel,
        out_shape=jax.ShapeDtypeStruct(own.shape, F32),
        in_specs=[pl.BlockSpec(memory_space=pltpu.VMEM)] * 3,
        out_specs=pl.BlockSpec(memory_space=pltpu.VMEM),
        compiler_params=pltpu.CompilerParams(vmem_limit_bytes=8 << 20),
        cost_estimate=COST,
        name="merge",
    )(own, received, row_map)


def update_kernel(
    core_ref, front_ref, panels_ref, near_ref, far_ref, lefts_ref, window_ref, inverse_ref, out_ref,
    high_ref, low_ref, other_high_ref, other_low_ref, *, tiles,
):
    levels, rows, width = window_ref.shape
    top = lefts_ref.shape[1]

    @pl.when(pl.program_id(0) == 0)
    def _():
        for level in range(levels):
            cols = slice(level * width, (level + 1) * width)
            inverse = split2(inverse_ref[level])
            left = jnp.concatenate([lefts_ref[level], window_ref[level, top:]], axis=0)
            high_ref[:, cols], low_ref[:, cols] = split2(product2_nt(split2(left), inverse))
            if level == 0:
                solved = product2_nt(split2(lefts_ref[levels]), inverse)
                other_high_ref[...], other_low_ref[...] = split2(solved)

    columns = jnp.concatenate([panels_ref[level] for level in range(levels)], axis=1)
    update = product2_nt((high_ref[...], low_ref[...]), split2(columns))
    half = pl.program_id(0) // (tiles // 2)
    other = jnp.where(half == core_ref[0], near_ref[...], far_ref[...])
    other = product2_nt((other_high_ref[...], other_low_ref[...]), split2(other))
    out_ref[:top] = -update[:top] - other
    out_ref[top:] = front_ref[top:] - update[top:]


def updated_rows(core, front, panels, near, far, lefts, window, inverse):
    rows, cols = front.shape
    top = lefts.shape[1]
    levels, _, width = panels.shape
    tile = 256
    tiles = cols // tile
    whole = lambda x: pl.BlockSpec(x.shape, lambda j, core: (0,) * x.ndim)
    half = pl.BlockSpec((tile, width), lambda j, core: (lax.rem(j, tiles // 2), 0))
    wide = pltpu.VMEM((rows, levels * width), BF16)
    other = pltpu.VMEM((top, width), BF16)
    return pl.pallas_call(
        functools.partial(update_kernel, tiles=tiles),
        grid_spec=pltpu.PrefetchScalarGridSpec(
            num_scalar_prefetch=1,
            grid=(tiles,),
            in_specs=[
                pl.BlockSpec((rows, tile), lambda j, core: (0, j)),
                pl.BlockSpec((levels, tile, width), lambda j, core: (0, j, 0)),
                half,
                half,
                whole(lefts),
                whole(window),
                whole(inverse),
            ],
            out_specs=pl.BlockSpec((rows, tile), lambda j, core: (0, j)),
            scratch_shapes=[wide, wide, other, other],
        ),
        out_shape=jax.ShapeDtypeStruct(front.shape, F32),
        compiler_params=pltpu.CompilerParams(vmem_limit_bytes=24 << 20),
        cost_estimate=COST,
        name="updated_rows",
    )(core, front, panels, near, far, lefts, window, inverse)


def finish_kernel(own_ref, received_ref, map_ref, rest_ref, out_ref):
    out_ref[...] = own_ref[...] + moved(received_ref[...], map_ref[...]) + rest_ref[...]


def finished(own, received, row_map, updated, part):
    rows, cols = own.shape
    steps = 2
    tile = cols // steps
    block = pl.BlockSpec((rows, tile), lambda j: (0, j))
    placed = pl.BlockSpec((rows, tile), lambda j: (0, part * steps + j))
    return pl.pallas_call(
        finish_kernel,
        grid=(steps,),
        in_specs=[block, block, pl.BlockSpec((1, rows), lambda j: (0, 0)), placed],
        out_specs=placed,
        out_shape=jax.ShapeDtypeStruct(updated.shape, F32),
        input_output_aliases={3: 0},
        compiler_params=pltpu.CompilerParams(vmem_limit_bytes=8 << 20),
        cost_estimate=COST,
        name="finished",
    )(own, received, row_map, updated)


def partner(x, axis, flip):
    return lax.ppermute(x, axis, [(i, i ^ flip) for i in range(lax.axis_size(axis))])


def after(x, *earlier):
    return lax.optimization_barrier((x, *earlier))[0]


def to_all(x, axis, flips=None):
    if flips is None:
        flips = [1 << bit for bit in range(lax.axis_size(axis).bit_length() - 1)]
    groups = []
    for start in range(lax.axis_size(axis)):
        group = [start]
        for flip in flips:
            group += [index ^ flip for index in group]
        if start == min(group):
            groups.append(sorted(group))
    copies = jnp.broadcast_to(x[None], (len(groups[0]), *x.shape))
    return lax.all_to_all(copies, axis, 0, 0, tiled=True, axis_index_groups=groups)


def dealt(parts, axis, sizes):
    count = parts.shape[0]

    def place(index):
        found = []
        for size in reversed(sizes):
            found.append(index % size)
            index //= size
        return found

    def distance(a, b):
        steps = [(abs(i - j), size) for i, j, size in zip(place(a), place(b), reversed(sizes))]
        return sum(min(step, size - step) for step, size in steps)

    holders = [index for index in range(count) if sum(place(index)) <= 1]
    most = -(-count // len(holders))
    shares = {holder: [holder] for holder in holders}
    for index in sorted(range(count), key=lambda i: (-distance(i, 0), i)):
        if index not in holders:
            free = [h for h in holders if len(shares[h]) < most]
            shares[min(free, key=lambda h: (distance(h, index), len(shares[h])))].append(index)
    for share in shares.values():
        share += [share[0]] * (most - len(share))

    device = lax.axis_index(axis)
    held = [
        lax.ppermute(jnp.stack([parts[i] for i in shares[holder]]), axis, [(0, holder)])
        for holder in holders if holder
    ]

    def rest(held):
        first = jnp.stack([parts[i] for i in shares[0]])
        held = jnp.where(device == 0, first, functools.reduce(jnp.add, held))
        received = [held[0]]
        for slot in range(1, most):
            pairs = [(h, share[slot]) for h, share in shares.items() if share[slot] != h]
            received.append(lax.ppermute(held[slot], axis, pairs))
        is_holder = functools.reduce(jnp.logical_or, [device == h for h in holders])
        return jnp.where(is_holder, received[0], functools.reduce(jnp.add, received[1:]))

    return held, rest


def body(front, panels, diagonal_blocks, extend_maps):
    rows, cols = front.shape
    levels, _, width = panels.shape
    top = extend_maps.shape[3]
    row_index = lax.axis_index("fr")
    row_devices, col_devices = lax.axis_size("fr"), lax.axis_size("fc")
    maps = [extend_maps[l, 0] for l in range(levels)]
    flips = [("fc", col_devices // 2), ("fc", 1), ("fr", row_devices // 2), ("fr", 1)]
    core = row_index % 2
    half = cols // 2

    own_a, own_b = front[:top, :half], front[:top, half:]
    received_a = partner(own_a, *flips[0])

    own = lax.dynamic_slice_in_dim(panels, row_index * rows, rows, 1)
    held, rest = dealt(own.reshape(col_devices, -1, width), "fc", (4, 2, 4))
    near = lax.dynamic_slice_in_dim(panels[0], core * half, half, 0)
    near = partner(near, "fc", 1)
    gathered = to_all(jnp.swapaxes(diagonal_blocks, 1, 2), "fc")

    merged_a = merge(own_a, received_a, maps[0])
    received_a = partner(merged_a, *flips[1])
    received_b = partner(after(own_b, merged_a), *flips[0])
    part = rest(after(held, merged_a))
    part = to_all(part, "fc", [1, 2, 4])
    window = to_all(part, "fc", [8, 16])
    inverse = inverses(after(gathered, part, merged_a))
    far = partner(near, "fr", 1)

    merged_b = merge(own_b, after(received_b, inverse), maps[0])
    merged_a = merge(merged_a, after(received_a, inverse), maps[1])
    received_b = partner(merged_b, *flips[1])
    received_a = partner(merged_a, *flips[2])

    window = after(window, merged_a, merged_b).reshape(levels, rows, width)
    first = window[:, :top]
    turned = jnp.take(first[0], maps[1][0], axis=0, mode="clip")
    lefts = jnp.concatenate([first[0], first[1], turned], axis=1)
    lefts = merge(lefts, partner(lefts, *flips[2]), maps[2])
    lefts = jnp.concatenate([lefts, first[2]], axis=1)
    lefts = merge(lefts, partner(lefts, *flips[3]), maps[3])
    zero, one, other, two = [lefts[:, i * width:(i + 1) * width] for i in range(4)]
    lefts = jnp.stack([zero, one, two, first[3], other])

    merged_b = merge(merged_b, received_b, maps[1])
    merged_a = merge(merged_a, received_a, maps[2])
    received_b = partner(merged_b, *flips[2])
    received_a = partner(merged_a, *flips[3])

    updated = updated_rows(
        core[None], front, panels, near, far, after(lefts, merged_a, merged_b), window, inverse)

    merged_b = merge(merged_b, after(received_b, updated), maps[2])
    received_b = partner(merged_b, *flips[3])
    updated = finished(merged_a, received_a, maps[3], updated, 0)
    return finished(merged_b, received_b, maps[3], updated, 1)

def solution(mesh):
    in_specs = (P("fr", "fc"), P(None, "fc", None), P(None, None, "fc"), P(None, "fr", "fc", None))
    out_specs = P("fr", "fc")
    return jax.shard_map(body, mesh=mesh, in_specs=in_specs, out_specs=out_specs, check_vma=False)
```

```python
import functools

import jax
import jax.numpy as jnp
from jax import lax
from jax.experimental import pallas as pl
from jax.experimental.pallas import tpu as pltpu
from jax.sharding import PartitionSpec as P

BF16, F32 = jnp.bfloat16, jnp.float32
COST = pl.CostEstimate(flops=1, bytes_accessed=1, transcendentals=0)

def split3(x):
    hi = x.astype(BF16)
    rest = x - hi.astype(F32)
    mid = rest.astype(BF16)
    low = (rest - mid.astype(F32)).astype(BF16)
    return hi, mid, low

def dot_nt(a, b):
    return lax.dot_general(a, b, (((1,), (1,)), ((), ())), preferred_element_type=F32)

def product_nt(a, b):
    ah, am, al = split3(a)
    bh, bm, bl = split3(b)
    cat = lambda x, y: jnp.concatenate([x, y], axis=1)
    small = dot_nt(cat(am, ah), cat(bm, bl)) + dot_nt(cat(al, am), cat(bh, bh))
    return dot_nt(cat(ah, ah), cat(bh, bm)) + small

def sweep_block(block, width):
    rows, lanes = block.shape
    row = lax.broadcasted_iota(jnp.int32, (rows, lanes), 0)
    lane = lax.broadcasted_iota(jnp.int32, (rows, lanes), 1)
    own = lane % width
    group = lane - own
    own1 = own[:1]
    for p in range(0, rows, 2):
        c0 = jnp.take_along_axis(block, group + p, axis=1)
        c1 = jnp.take_along_axis(block, group + (p + 1), axis=1)
        d00, d01, d11 = c0[p:p + 1], c0[p + 1:p + 2], c1[p + 1:p + 2]
        r0 = jnp.where(own1 == p, -1.0, jnp.where(own1 == p + 1, 0.0, block[p:p + 1]))
        r1 = jnp.where(own1 == p + 1, -1.0, jnp.where(own1 == p, 0.0, block[p + 1:p + 2]))
        scale = 1.0 / (d00 * d11 - d01 * d01)
        u0 = (d11 * r0 - d01 * r1) * scale
        u1 = (d00 * r1 - d01 * r0) * scale
        at0, at1 = row == p, row == p + 1
        c0 = jnp.where(at0, -1.0, jnp.where(at1, 0.0, c0))
        c1 = jnp.where(at1, -1.0, jnp.where(at0, 0.0, c1))
        pivot = at0 | at1 | (own == p) | (own == p + 1)
        block = jnp.where(pivot, 0.0, block) - c0 * u0 - c1 * u1
    return block

def inverse_kernel(gathered_ref, inverse_ref, packed_ref, *, width):
    levels, order = inverse_ref.shape[0], inverse_ref.shape[1]
    lanes = levels * width
    blocks = order // width
    per_tile = lanes // width
    lane_group = lax.broadcasted_iota(jnp.int32, (order, lanes), 1) // width
    for level in range(levels):
        rows = gathered_ref[:, level].reshape(order, order)
        symmetric = 0.5 * (rows + rows.T)
        for b in range(blocks):
            tile, place = divmod(b, per_tile)
            piece = symmetric[:, tile * lanes:(tile + 1) * lanes]
            shift = (level - place) * width % lanes
            if shift:
                piece = pltpu.roll(piece, shift, 1)
            cols = slice(b * lanes, (b + 1) * lanes)
            if level == 0:
                packed_ref[:, cols] = piece
            else:
                packed_ref[:, cols] = jnp.where(lane_group == level, piece, packed_ref[:, cols])
    same = (lax.broadcasted_iota(jnp.int32, (lanes, lanes), 0) // width
            == lax.broadcasted_iota(jnp.int32, (lanes, lanes), 1) // width)
    small_row = lax.broadcasted_iota(jnp.int32, (width, lanes), 0)
    small_own = lax.broadcasted_iota(jnp.int32, (width, lanes), 1) % width
    minus_identity = jnp.where(small_row == small_own, -1.0, 0.0)

    def spread(x):
        return jnp.where(same, jnp.concatenate([x] * levels, axis=0), 0.0)

    def step(b, carry):
        cols = pl.ds(pl.multiple_of(b * lanes, lanes), lanes)
        rows = pl.ds(pl.multiple_of(b * width, width), width)
        negated = sweep_block(packed_ref[rows, cols], width)
        packed_ref[rows, :] = jnp.zeros((width, blocks * lanes), F32)
        packed_ref[rows, cols] = minus_identity
        column = packed_ref[:, cols]
        packed_ref[:, cols] = jnp.zeros((order, lanes), F32)
        scaled = product_nt(column, spread(negated))
        wide = jnp.concatenate(
            [spread(column[i * width:(i + 1) * width]) for i in range(blocks)], axis=0)
        packed_ref[...] += product_nt(scaled, wide)
        return carry

    lax.fori_loop(0, blocks, step, 0)
    for level in range(levels):
        for tile in range(order // lanes):
            total = None
            for place in range(per_tile):
                b = tile * per_tile + place
                piece = packed_ref[:, b * lanes:(b + 1) * lanes]
                shift = (place - level) * width % lanes
                if shift:
                    piece = pltpu.roll(piece, shift, 1)
                total = piece if total is None else jnp.where(lane_group == place, piece, total)
            inverse_ref[level, :, tile * lanes:(tile + 1) * lanes] = -total

def inverses(gathered):
    parts, levels, eight, order = gathered.shape
    width = 32
    return pl.pallas_call(
        functools.partial(inverse_kernel, width=width),
        out_shape=jax.ShapeDtypeStruct((levels, order, order), F32),
        in_specs=[pl.BlockSpec(memory_space=pltpu.VMEM)],
        out_specs=pl.BlockSpec(memory_space=pltpu.VMEM),
        scratch_shapes=[pltpu.VMEM((order, levels * order), F32)],
        compiler_params=pltpu.CompilerParams(vmem_limit_bytes=16 << 20),
        cost_estimate=COST,
        name="symmetric_inverses",
    )(gathered)


def split2(x):
    high = x.astype(BF16)
    return high, (x - high.astype(F32)).astype(BF16)


def product2_nt(a, b):
    return dot_nt(a[0], b[0]) + (dot_nt(a[0], b[1]) + dot_nt(a[1], b[0]))


def moved(x, row_map):
    rows = x.shape[0]
    pick = lax.broadcasted_iota(jnp.int32, (rows, rows), 0) == row_map
    pick = jnp.where(pick, 1.0, 0.0).T.astype(BF16)
    high, mid, low = (jnp.dot(pick, part, preferred_element_type=F32) for part in split3(x))
    return (high + mid) + low


def merge_kernel(own_ref, received_ref, map_ref, out_ref):
    step = 256
    for start in range(0, out_ref.shape[1], step):
        cols = slice(start, start + step)
        out_ref[:, cols] = own_ref[:, cols] + moved(received_ref[:, cols], map_ref[...])


def merge(own, received, row_map):
    return pl.pallas_call(
        merge_kernel,
        out_shape=jax.ShapeDtypeStruct(own.shape, F32),
        in_specs=[pl.BlockSpec(memory_space=pltpu.VMEM)] * 3,
        out_specs=pl.BlockSpec(memory_space=pltpu.VMEM),
        compiler_params=pltpu.CompilerParams(vmem_limit_bytes=8 << 20),
        cost_estimate=COST,
        name="merge",
    )(own, received, row_map)


def solve(left, inverse, stacked_ref, index):
    rows, width = left.shape
    cols = slice(index * width, (index + 1) * width)
    high, low = split2(product2_nt(split2(left), split2(inverse)))
    stacked_ref[:rows, cols] = high
    stacked_ref[rows:, cols] = low


def stacked_product(stacked_ref, columns):
    rows = stacked_ref.shape[0] // 2
    high, low = split2(columns)
    both = dot_nt(stacked_ref[...], high)
    return both[:rows] + (both[rows:] + dot_nt(stacked_ref[:rows], low))


def lower_kernel(front_ref, panels_ref, window_ref, inverse_ref, out_ref, stacked_ref):
    levels = window_ref.shape[0]
    top = out_ref.shape[0] - stacked_ref.shape[0] // 2

    @pl.when(pl.program_id(0) == 0)
    def _():
        for level in range(levels):
            solve(window_ref[level, top:], inverse_ref[level], stacked_ref, level)

    columns = jnp.concatenate([panels_ref[level] for level in range(levels)], axis=1)
    out_ref[:top] = front_ref[:top]
    out_ref[top:] = front_ref[top:] - stacked_product(stacked_ref, columns)


def lower_rows(front, panels, window, inverse, top):
    rows, cols = front.shape
    levels, _, width = panels.shape
    tile = 256
    whole = lambda x: pl.BlockSpec(x.shape, lambda j: (0,) * x.ndim)
    return pl.pallas_call(
        lower_kernel,
        grid=(cols // tile,),
        in_specs=[
            pl.BlockSpec((rows, tile), lambda j: (0, j)),
            pl.BlockSpec((levels, tile, width), lambda j: (0, j, 0)),
            whole(window),
            whole(inverse),
        ],
        out_specs=pl.BlockSpec((rows, tile), lambda j: (0, j)),
        scratch_shapes=[pltpu.VMEM((2 * (rows - top), levels * width), BF16)],
        out_shape=jax.ShapeDtypeStruct(front.shape, F32),
        compiler_params=pltpu.CompilerParams(vmem_limit_bytes=24 << 20),
        cost_estimate=COST,
        name="lower_rows",
    )(front, panels, window, inverse)


def upper_kernel(
    core_ref, panels_ref, near_ref, far_ref, lefts_ref, inverse_ref, lower_ref, out_ref, stacked_ref, *, tiles,
):
    del lower_ref
    levels = panels_ref.shape[0]

    @pl.when(pl.program_id(0) == 0)
    def _():
        for index in range(levels + 1):
            solve(lefts_ref[index], inverse_ref[index % levels], stacked_ref, index)

    half = pl.program_id(0) // (tiles // 2)
    other = jnp.where(half == core_ref[0], near_ref[...], far_ref[...])
    columns = jnp.concatenate([panels_ref[level] for level in range(levels)] + [other], axis=1)
    out_ref[...] = -stacked_product(stacked_ref, columns)


def upper_rows(core, panels, near, far, lefts, inverse, lower):
    levels, cols, width = panels.shape
    rows = lefts.shape[1]
    tile = 512
    tiles = cols // tile
    half = pl.BlockSpec((tile, width), lambda j, core: (lax.rem(j, tiles // 2), 0))
    whole = lambda x: pl.BlockSpec(x.shape, lambda j, core: (0,) * x.ndim)
    return pl.pallas_call(
        functools.partial(upper_kernel, tiles=tiles),
        grid_spec=pltpu.PrefetchScalarGridSpec(
            num_scalar_prefetch=1,
            grid=(tiles,),
            in_specs=[
                pl.BlockSpec((levels, tile, width), lambda j, core: (0, j, 0)),
                half,
                half,
                whole(lefts),
                whole(inverse),
                pl.BlockSpec(memory_space=pl.ANY),
            ],
            out_specs=pl.BlockSpec((rows, tile), lambda j, core: (0, j)),
            scratch_shapes=[pltpu.VMEM((2 * rows, (levels + 1) * width), BF16)],
        ),
        out_shape=jax.ShapeDtypeStruct(lower.shape, F32),
        input_output_aliases={6: 0},
        compiler_params=pltpu.CompilerParams(vmem_limit_bytes=24 << 20),
        cost_estimate=COST,
        name="upper_rows",
    )(core, panels, near, far, lefts, inverse, lower)


def finish_kernel(own_ref, received_ref, map_ref, rest_ref, out_ref):
    out_ref[...] = own_ref[...] + moved(received_ref[...], map_ref[...]) + rest_ref[...]


def finished(own, received, row_map, updated, part):
    rows, cols = own.shape
    steps = 2
    tile = cols // steps
    block = pl.BlockSpec((rows, tile), lambda j: (0, j))
    placed = pl.BlockSpec((rows, tile), lambda j: (0, part * steps + j))
    return pl.pallas_call(
        finish_kernel,
        grid=(steps,),
        in_specs=[block, block, pl.BlockSpec((1, rows), lambda j: (0, 0)), placed],
        out_specs=placed,
        out_shape=jax.ShapeDtypeStruct(updated.shape, F32),
        input_output_aliases={3: 0},
        compiler_params=pltpu.CompilerParams(vmem_limit_bytes=8 << 20),
        cost_estimate=COST,
        name="finished",
    )(own, received, row_map, updated)


def partner(x, axis, flip):
    return lax.ppermute(x, axis, [(i, i ^ flip) for i in range(lax.axis_size(axis))])


def after(x, *earlier):
    return lax.optimization_barrier((x, *earlier))[0]


def to_all(x, axis, flips=None):
    if flips is None:
        flips = [1 << bit for bit in range(lax.axis_size(axis).bit_length() - 1)]
    groups = []
    for start in range(lax.axis_size(axis)):
        group = [start]
        for flip in flips:
            group += [index ^ flip for index in group]
        if start == min(group):
            groups.append(sorted(group))
    copies = jnp.broadcast_to(x[None], (len(groups[0]), *x.shape))
    return lax.all_to_all(copies, axis, 0, 0, tiled=True, axis_index_groups=groups)


def dealt(parts, axis):
    runs, each = len(parts), parts[0].shape[0]
    first = [0, each // 2 - 1, each // 2, 1]
    device = lax.axis_index(axis)
    received = [lax.ppermute(parts[i], axis, [(0, first[i])]) for i in range(1, runs)]

    def deal_on(earlier):
        held = functools.reduce(jnp.add, after(received, earlier))
        held = jnp.where(device == 0, parts[0], held)
        pieces = [held[0]]
        for slot in range(each):
            pairs = [(first[i], i * each + slot) for i in range(runs) if first[i] != i * each + slot]
            pieces.append(lax.ppermute(held[slot], axis, pairs))
        return whole, pieces

    def whole(pieces):
        keeps = functools.reduce(
            jnp.logical_or, [device == first[i] for i in range(runs) if first[i] == i * each])
        return jnp.where(keeps, pieces[0], functools.reduce(jnp.add, pieces[1:]))

    return deal_on


def body(front, panels, diagonal_blocks, extend_maps):
    rows, cols = front.shape
    levels, _, width = panels.shape
    top = extend_maps.shape[3]
    row_index = lax.axis_index("fr")
    row_devices, col_devices = lax.axis_size("fr"), lax.axis_size("fc")
    maps = [extend_maps[l, 0] for l in range(levels)]
    flips = [("fc", col_devices // 2), ("fc", 1), ("fr", row_devices // 2), ("fr", 1)]
    core = row_index % 2
    stored = pltpu.with_memory_space_constraint(panels, pltpu.HBM)
    stored_front = pltpu.with_memory_space_constraint(front, pltpu.HBM)
    half = cols // 2

    own_a, own_b = front[:top, :half], front[:top, half:]
    received_a = partner(own_a, *flips[0])
    diagonal_part = after(jnp.swapaxes(diagonal_blocks, 1, 2), own_a)
    gathered = to_all(diagonal_part, "fc")

    first_row = after(row_index, own_a) * rows
    own = [
        lax.dynamic_slice(panels, (level, first_row, 0), (1, rows, width))
        .reshape(col_devices // levels, -1, width)
        for level in range(levels)
    ]
    deal_on = dealt(own, "fc")

    merged_a = merge(own_a, received_a, maps[0])
    received_a = partner(merged_a, *flips[1])
    received_b = partner(after(own_b, merged_a), *flips[0])
    whole_part, pieces = deal_on(merged_a)
    part = to_all(whole_part(pieces), "fc", [1, 2, 4])

    near = lax.dynamic_slice(panels, (0, core * half, 0), (1, half, width))[0]
    near = partner(after(near, part), "fc", 1)
    window = to_all(part, "fc", [8, 16])
    inverse = inverses(after(gathered, part, merged_a))
    far = partner(near, "fr", 1)

    merged_b = merge(own_b, after(received_b, inverse), maps[0])
    merged_a = merge(merged_a, after(received_a, inverse), maps[1])
    received_b = partner(merged_b, *flips[1])
    received_a = partner(merged_a, *flips[2])

    window = after(window, merged_a, merged_b).reshape(levels, rows, width)
    first = window[:, :top]
    turned = jnp.take(first[0], maps[1][0], axis=0, mode="clip")
    lefts = jnp.concatenate([first[0], first[1], turned], axis=1)
    lefts_received = partner(lefts, *flips[2])

    lower = lower_rows(stored_front, stored, after(window, lefts), inverse, top)

    merged_b = merge(merged_b, after(received_b, lower), maps[1])
    merged_a = merge(merged_a, after(received_a, lower), maps[2])
    received_b = partner(merged_b, *flips[2])
    received_a = partner(merged_a, *flips[3])

    lefts = merge(lefts, after(lefts_received, merged_a, merged_b), maps[2])
    lefts = jnp.concatenate([lefts, first[2]], axis=1)
    lefts = merge(lefts, partner(lefts, *flips[3]), maps[3])
    zero, one, other, two = [lefts[:, i * width:(i + 1) * width] for i in range(4)]
    lefts = jnp.stack([zero, one, two, first[3], other])

    updated = upper_rows(core[None], stored, near, far, lefts, inverse, lower)

    merged_b = merge(merged_b, after(received_b, updated), maps[2])
    received_b = partner(merged_b, *flips[3])
    updated = finished(merged_a, received_a, maps[3], updated, 0)
    return finished(merged_b, received_b, maps[3], updated, 1)

def solution(mesh):
    in_specs = (P("fr", "fc"), P(None, "fc", None), P(None, None, "fc"), P(None, "fr", "fc", None))
    out_specs = P("fr", "fc")
    return jax.shard_map(body, mesh=mesh, in_specs=in_specs, out_specs=out_specs, check_vma=False)
```

```python
import functools

import jax
import jax.numpy as jnp
from jax import lax
from jax.experimental import pallas as pl
from jax.experimental.pallas import tpu as pltpu
from jax.sharding import PartitionSpec as P

BF16, F32 = jnp.bfloat16, jnp.float32
COST = pl.CostEstimate(flops=1, bytes_accessed=1, transcendentals=0)

def split3(x):
    hi = x.astype(BF16)
    rest = x - hi.astype(F32)
    mid = rest.astype(BF16)
    low = (rest - mid.astype(F32)).astype(BF16)
    return hi, mid, low

def dot_nt(a, b):
    return lax.dot_general(a, b, (((1,), (1,)), ((), ())), preferred_element_type=F32)

def product_nt(a, b):
    ah, am, al = split3(a)
    bh, bm, bl = split3(b)
    cat = lambda x, y: jnp.concatenate([x, y], axis=1)
    small = dot_nt(cat(am, ah), cat(bm, bl)) + dot_nt(cat(al, am), cat(bh, bh))
    return dot_nt(cat(ah, ah), cat(bh, bm)) + small

def sweep_block(block, width):
    rows, lanes = block.shape
    row = lax.broadcasted_iota(jnp.int32, (rows, lanes), 0)
    lane = lax.broadcasted_iota(jnp.int32, (rows, lanes), 1)
    own = lane % width
    group = lane - own
    own1 = own[:1]
    for p in range(0, rows, 2):
        c0 = jnp.take_along_axis(block, group + p, axis=1)
        c1 = jnp.take_along_axis(block, group + (p + 1), axis=1)
        d00, d01, d11 = c0[p:p + 1], c0[p + 1:p + 2], c1[p + 1:p + 2]
        r0 = jnp.where(own1 == p, -1.0, jnp.where(own1 == p + 1, 0.0, block[p:p + 1]))
        r1 = jnp.where(own1 == p + 1, -1.0, jnp.where(own1 == p, 0.0, block[p + 1:p + 2]))
        scale = 1.0 / (d00 * d11 - d01 * d01)
        u0 = (d11 * r0 - d01 * r1) * scale
        u1 = (d00 * r1 - d01 * r0) * scale
        at0, at1 = row == p, row == p + 1
        c0 = jnp.where(at0, -1.0, jnp.where(at1, 0.0, c0))
        c1 = jnp.where(at1, -1.0, jnp.where(at0, 0.0, c1))
        pivot = at0 | at1 | (own == p) | (own == p + 1)
        block = jnp.where(pivot, 0.0, block) - c0 * u0 - c1 * u1
    return block

def inverse_kernel(gathered_ref, inverse_ref, packed_ref, *, width):
    levels, order = inverse_ref.shape[0], inverse_ref.shape[1]
    lanes = levels * width
    blocks = order // width
    per_tile = lanes // width
    lane_group = lax.broadcasted_iota(jnp.int32, (order, lanes), 1) // width
    for level in range(levels):
        rows = gathered_ref[:, level].reshape(order, order)
        symmetric = 0.5 * (rows + rows.T)
        for b in range(blocks):
            tile, place = divmod(b, per_tile)
            piece = symmetric[:, tile * lanes:(tile + 1) * lanes]
            shift = (level - place) * width % lanes
            if shift:
                piece = pltpu.roll(piece, shift, 1)
            cols = slice(b * lanes, (b + 1) * lanes)
            if level == 0:
                packed_ref[:, cols] = piece
            else:
                packed_ref[:, cols] = jnp.where(lane_group == level, piece, packed_ref[:, cols])
    same = (lax.broadcasted_iota(jnp.int32, (lanes, lanes), 0) // width
            == lax.broadcasted_iota(jnp.int32, (lanes, lanes), 1) // width)
    small_row = lax.broadcasted_iota(jnp.int32, (width, lanes), 0)
    small_own = lax.broadcasted_iota(jnp.int32, (width, lanes), 1) % width
    minus_identity = jnp.where(small_row == small_own, -1.0, 0.0)

    def spread(x):
        return jnp.where(same, jnp.concatenate([x] * levels, axis=0), 0.0)

    def step(b, carry):
        cols = pl.ds(pl.multiple_of(b * lanes, lanes), lanes)
        rows = pl.ds(pl.multiple_of(b * width, width), width)
        negated = sweep_block(packed_ref[rows, cols], width)
        packed_ref[rows, :] = jnp.zeros((width, blocks * lanes), F32)
        packed_ref[rows, cols] = minus_identity
        column = packed_ref[:, cols]
        packed_ref[:, cols] = jnp.zeros((order, lanes), F32)
        scaled = product_nt(column, spread(negated))
        wide = jnp.concatenate(
            [spread(column[i * width:(i + 1) * width]) for i in range(blocks)], axis=0)
        packed_ref[...] += product_nt(scaled, wide)
        return carry

    lax.fori_loop(0, blocks, step, 0)
    for level in range(levels):
        for tile in range(order // lanes):
            total = None
            for place in range(per_tile):
                b = tile * per_tile + place
                piece = packed_ref[:, b * lanes:(b + 1) * lanes]
                shift = (place - level) * width % lanes
                if shift:
                    piece = pltpu.roll(piece, shift, 1)
                total = piece if total is None else jnp.where(lane_group == place, piece, total)
            inverse_ref[level, :, tile * lanes:(tile + 1) * lanes] = -total

def inverses(gathered):
    parts, levels, eight, order = gathered.shape
    width = 32
    return pl.pallas_call(
        functools.partial(inverse_kernel, width=width),
        out_shape=jax.ShapeDtypeStruct((levels, order, order), F32),
        in_specs=[pl.BlockSpec(memory_space=pltpu.VMEM)],
        out_specs=pl.BlockSpec(memory_space=pltpu.VMEM),
        scratch_shapes=[pltpu.VMEM((order, levels * order), F32)],
        compiler_params=pltpu.CompilerParams(vmem_limit_bytes=16 << 20),
        cost_estimate=COST,
        name="symmetric_inverses",
    )(gathered)


def split2(x):
    high = x.astype(BF16)
    return high, (x - high.astype(F32)).astype(BF16)


def product2_nt(a, b):
    return dot_nt(a[0], b[0]) + (dot_nt(a[0], b[1]) + dot_nt(a[1], b[0]))


def moved(x, row_map):
    rows = x.shape[0]
    pick = lax.broadcasted_iota(jnp.int32, (rows, rows), 0) == row_map
    pick = jnp.where(pick, 1.0, 0.0).T.astype(BF16)
    high, mid, low = (jnp.dot(pick, part, preferred_element_type=F32) for part in split3(x))
    return (high + mid) + low


def merge_kernel(own_ref, received_ref, map_ref, out_ref):
    step = 256
    for start in range(0, out_ref.shape[1], step):
        cols = slice(start, start + step)
        out_ref[:, cols] = own_ref[:, cols] + moved(received_ref[:, cols], map_ref[...])


def merge(own, received, row_map):
    return pl.pallas_call(
        merge_kernel,
        out_shape=jax.ShapeDtypeStruct(own.shape, F32),
        in_specs=[pl.BlockSpec(memory_space=pltpu.VMEM)] * 3,
        out_specs=pl.BlockSpec(memory_space=pltpu.VMEM),
        compiler_params=pltpu.CompilerParams(vmem_limit_bytes=8 << 20),
        cost_estimate=COST,
        name="merge",
    )(own, received, row_map)


def solve(left, inverse, stacked_ref, index):
    rows, width = left.shape
    cols = slice(index * width, (index + 1) * width)
    high, low = split2(product2_nt(split2(left), split2(inverse)))
    stacked_ref[:rows, cols] = high
    stacked_ref[rows:, cols] = low


def stacked_product(stacked_ref, columns):
    rows = stacked_ref.shape[0] // 2
    high, low = split2(columns)
    both = dot_nt(stacked_ref[...], high)
    return both[:rows] + (both[rows:] + dot_nt(stacked_ref[:rows], low))


def lower_kernel(front_ref, panels_ref, window_ref, inverse_ref, *rest):
    out_ref, stacked_ref = rest[-2:]
    levels = window_ref.shape[0]
    top = out_ref.shape[0] - stacked_ref.shape[0] // 2

    @pl.when(pl.program_id(0) == 0)
    def _():
        for level in range(levels):
            solve(window_ref[level, top:], inverse_ref[level], stacked_ref, level)

    columns = jnp.concatenate([panels_ref[level] for level in range(levels)], axis=1)
    out_ref[:top] = front_ref[:top]
    out_ref[top:] = front_ref[top:] - stacked_product(stacked_ref, columns)


def lower_rows(front, panels, window, inverse, top, part, into=None):
    rows, cols = front.shape
    levels, _, width = panels.shape
    tile = 256
    tiles = cols // tile // 2
    skip = part * tiles
    extra = [] if into is None else [into]
    whole = lambda x: pl.BlockSpec(x.shape, lambda j: (0,) * x.ndim)
    return pl.pallas_call(
        lower_kernel,
        grid=(tiles,),
        in_specs=[
            pl.BlockSpec((rows, tile), lambda j: (0, skip + j)),
            pl.BlockSpec((levels, tile, width), lambda j: (0, skip + j, 0)),
            whole(window),
            whole(inverse),
        ] + [pl.BlockSpec(memory_space=pl.ANY)] * len(extra),
        out_specs=pl.BlockSpec((rows, tile), lambda j: (0, skip + j)),
        scratch_shapes=[pltpu.VMEM((2 * (rows - top), levels * width), BF16)],
        out_shape=jax.ShapeDtypeStruct(front.shape, F32),
        input_output_aliases={4: 0} if extra else {},
        compiler_params=pltpu.CompilerParams(vmem_limit_bytes=24 << 20),
        cost_estimate=COST,
        name="lower_rows",
    )(front, panels, window, inverse, *extra)


def upper_kernel(
    core_ref, panels_ref, near_ref, far_ref, lefts_ref, inverse_ref, lower_ref, out_ref, stacked_ref, *, tiles,
):
    del lower_ref
    levels = panels_ref.shape[0]

    @pl.when(pl.program_id(0) == 0)
    def _():
        for index in range(levels + 1):
            solve(lefts_ref[index], inverse_ref[index % levels], stacked_ref, index)

    half = pl.program_id(0) // (tiles // 2)
    other = jnp.where(half == core_ref[0], near_ref[...], far_ref[...])
    columns = jnp.concatenate([panels_ref[level] for level in range(levels)] + [other], axis=1)
    out_ref[...] = -stacked_product(stacked_ref, columns)


def upper_rows(core, panels, near, far, lefts, inverse, lower):
    levels, cols, width = panels.shape
    rows = lefts.shape[1]
    tile = 512
    tiles = cols // tile
    half = pl.BlockSpec((tile, width), lambda j, core: (lax.rem(j, tiles // 2), 0))
    whole = lambda x: pl.BlockSpec(x.shape, lambda j, core: (0,) * x.ndim)
    return pl.pallas_call(
        functools.partial(upper_kernel, tiles=tiles),
        grid_spec=pltpu.PrefetchScalarGridSpec(
            num_scalar_prefetch=1,
            grid=(tiles,),
            in_specs=[
                pl.BlockSpec((levels, tile, width), lambda j, core: (0, j, 0)),
                half,
                half,
                whole(lefts),
                whole(inverse),
                pl.BlockSpec(memory_space=pl.ANY),
            ],
            out_specs=pl.BlockSpec((rows, tile), lambda j, core: (0, j)),
            scratch_shapes=[pltpu.VMEM((2 * rows, (levels + 1) * width), BF16)],
        ),
        out_shape=jax.ShapeDtypeStruct(lower.shape, F32),
        input_output_aliases={6: 0},
        compiler_params=pltpu.CompilerParams(vmem_limit_bytes=24 << 20),
        cost_estimate=COST,
        name="upper_rows",
    )(core, panels, near, far, lefts, inverse, lower)


def finish_kernel(own_ref, received_ref, map_ref, rest_ref, out_ref):
    out_ref[...] = own_ref[...] + moved(received_ref[...], map_ref[...]) + rest_ref[...]


def finished(own, received, row_map, updated, part):
    rows, cols = own.shape
    steps = 2
    tile = cols // steps
    block = pl.BlockSpec((rows, tile), lambda j: (0, j))
    placed = pl.BlockSpec((rows, tile), lambda j: (0, part * steps + j))
    return pl.pallas_call(
        finish_kernel,
        grid=(steps,),
        in_specs=[block, block, pl.BlockSpec((1, rows), lambda j: (0, 0)), placed],
        out_specs=placed,
        out_shape=jax.ShapeDtypeStruct(updated.shape, F32),
        input_output_aliases={3: 0},
        compiler_params=pltpu.CompilerParams(vmem_limit_bytes=8 << 20),
        cost_estimate=COST,
        name="finished",
    )(own, received, row_map, updated)


def partner(x, axis, flip):
    return lax.ppermute(x, axis, [(i, i ^ flip) for i in range(lax.axis_size(axis))])


def after(x, *earlier):
    return lax.optimization_barrier((x, *earlier))[0]


def to_all(x, axis, flips=None):
    if flips is None:
        flips = [1 << bit for bit in range(lax.axis_size(axis).bit_length() - 1)]
    groups = []
    for start in range(lax.axis_size(axis)):
        group = [start]
        for flip in flips:
            group += [index ^ flip for index in group]
        if start == min(group):
            groups.append(sorted(group))
    copies = jnp.broadcast_to(x[None], (len(groups[0]), *x.shape))
    return lax.all_to_all(copies, axis, 0, 0, tiled=True, axis_index_groups=groups)


def dealt(parts, axis):
    runs, each = len(parts), parts[0].shape[0]
    first = [0, each // 2 - 1, each // 2, 1]
    device = lax.axis_index(axis)
    received = [lax.ppermute(parts[i], axis, [(0, first[i])]) for i in range(1, runs)]

    def deal_on(earlier):
        held = functools.reduce(jnp.add, after(received, earlier))
        held = jnp.where(device == 0, parts[0], held)
        pieces = [held[0]]
        for slot in range(each):
            pairs = [(first[i], i * each + slot) for i in range(runs) if first[i] != i * each + slot]
            pieces.append(lax.ppermute(held[slot], axis, pairs))
        return whole, pieces

    def whole(pieces):
        keeps = functools.reduce(
            jnp.logical_or, [device == first[i] for i in range(runs) if first[i] == i * each])
        return jnp.where(keeps, pieces[0], functools.reduce(jnp.add, pieces[1:]))

    return deal_on


def body(front, panels, diagonal_blocks, extend_maps):
    rows, cols = front.shape
    levels, _, width = panels.shape
    top = extend_maps.shape[3]
    row_index = lax.axis_index("fr")
    row_devices, col_devices = lax.axis_size("fr"), lax.axis_size("fc")
    maps = [extend_maps[l, 0] for l in range(levels)]
    flips = [("fc", col_devices // 2), ("fc", 1), ("fr", row_devices // 2), ("fr", 1)]
    core = row_index % 2
    stored = pltpu.with_memory_space_constraint(panels, pltpu.HBM)
    stored_front = pltpu.with_memory_space_constraint(front, pltpu.HBM)
    half = cols // 2

    own_a, own_b = front[:top, :half], front[:top, half:]
    received_a = partner(own_a, *flips[0])
    diagonal_part = after(jnp.swapaxes(diagonal_blocks, 1, 2), own_a)
    gathered = to_all(diagonal_part, "fc")

    first_row = after(row_index, own_a) * rows
    own = [
        lax.dynamic_slice(panels, (level, first_row, 0), (1, rows, width))
        .reshape(col_devices // levels, -1, width)
        for level in range(levels)
    ]
    deal_on = dealt(own, "fc")

    merged_a = merge(own_a, received_a, maps[0])
    received_a = partner(merged_a, *flips[1])
    received_b = partner(after(own_b, merged_a), *flips[0])
    whole_part, pieces = deal_on(merged_a)
    part = to_all(whole_part(pieces), "fc", [1, 2, 4])

    near = lax.dynamic_slice(panels, (0, core * half, 0), (1, half, width))[0]
    near = partner(after(near, part), "fc", 1)
    window = to_all(part, "fc", [8, 16])
    inverse = inverses(after(gathered, part, merged_a))
    far = partner(near, "fr", 1)

    merged_b = merge(own_b, after(received_b, inverse), maps[0])
    merged_a = merge(merged_a, after(received_a, inverse), maps[1])
    received_b = partner(merged_b, *flips[1])
    received_a = partner(merged_a, *flips[2])

    window = after(window, merged_a, merged_b).reshape(levels, rows, width)
    first = window[:, :top]
    turned = jnp.take(first[0], maps[1][0], axis=0, mode="clip")
    lefts = jnp.concatenate([first[0], first[1], turned], axis=1)
    lefts_received = partner(lefts, *flips[2])

    lower = lower_rows(stored_front, stored, after(window, lefts), inverse, top, 0)

    merged_b = merge(merged_b, after(received_b, lower), maps[1])
    merged_a = merge(merged_a, after(received_a, lower), maps[2])
    received_b = partner(merged_b, *flips[2])
    received_a = partner(merged_a, *flips[3])

    lower = lower_rows(
        stored_front, stored, after(window, merged_a, merged_b), inverse, top, 1, lower)

    lefts = merge(lefts, after(lefts_received, lower), maps[2])
    lefts = jnp.concatenate([lefts, first[2]], axis=1)
    lefts = merge(lefts, partner(lefts, *flips[3]), maps[3])
    zero, one, other, two = [lefts[:, i * width:(i + 1) * width] for i in range(4)]
    lefts = jnp.stack([zero, one, two, first[3], other])

    updated = upper_rows(core[None], stored, near, far, lefts, inverse, lower)

    merged_b = merge(merged_b, after(received_b, updated), maps[2])
    received_b = partner(merged_b, *flips[3])
    updated = finished(merged_a, received_a, maps[3], updated, 0)
    return finished(merged_b, received_b, maps[3], updated, 1)

def solution(mesh):
    in_specs = (P("fr", "fc"), P(None, "fc", None), P(None, None, "fc"), P(None, "fr", "fc", None))
    out_specs = P("fr", "fc")
    return jax.shard_map(body, mesh=mesh, in_specs=in_specs, out_specs=out_specs, check_vma=False)
```
